32 devices in a mesh: dp: 4 (over y, core), table: 8 (over z, x).
Axes of the slice: x: 2, y: 2, z: 4, core: 2. Of those that a mesh axis runs over, the one named last changes fastest.
Arguments:
- table: float32 [131072, 256], P(('dp', 'table')), may hold values from -6 to 6
- hidden: float32 [16384, 256], P(('dp', 'table')), may hold values from -24 to 24
- neg_ids: int32 [4, 8, 4, 128], P('dp', 'table'), may hold values from 0 to 4095
- pos_ids: int32 [16384], P(('dp', 'table')), may hold values from 0 to 4095
- dloss: float32 [16384], P(('dp', 'table')), may hold values from -4 to 4
Outputs:
- row_loss: float32 [16384], P(('dp', 'table'))
- grad_hidden: float32 [16384, 256], P(('dp', 'table'))
- grad_table: float32 [131072, 256], P(('dp', 'table'))
The draws below stay inside these ranges and needn't reach their ends.
All inputs are finite; a program needn't handle non-finite values.
Results may differ from the reference program's by a relative error of at most 0.0003.
Values sent between devices are 32-bit elements; how exact they have to be, the bound alone decides.
A program may use at most 192 MiB of HBM per device.

```python
import math
import jax
import jax.numpy as jnp
from jax import lax

D = 256
ROWS_DEV = 4096
NEG_PEER = 128
GROUP_ROWS = 4096
ROWS = 16384
ITEMS = 131072
POOL = 4096
N_DP = 4
N_TABLE = 8


def draw_table(key, part):
    noise_part = jax.random.normal(jax.random.fold_in(key, 21), (ITEMS, D), jnp.float32)
    return jnp.clip(noise_part, -4.0, 4.0)


def draw_hidden(key, part):
    noise_part = jax.random.normal(jax.random.fold_in(key, 31), (ROWS, D), jnp.float32)
    return jnp.clip(noise_part, -4.0, 4.0)


def place_ends(entries, stream_key, least, high):
    longest = entries.shape.index(max(entries.shape))
    spots = []
    for shift in (0, 1):
        where = [jax.random.randint(jax.random.fold_in(stream_key, axis), (), 0, length) for axis, length in enumerate(entries.shape)]
        where[longest] = (where[longest] + shift) % entries.shape[longest]
        spots.append(tuple(where))
    return entries.at[spots[0]].set(least).at[spots[1]].set(high)


def block_scale(key, extent, split, least, high):
    def one(position, parts):
        heights = jax.random.uniform(jax.random.fold_in(jax.random.fold_in(key, 6), position), (parts,), jnp.float32, least / len(split), high / len(split))
        return jnp.repeat(jnp.exp(heights), extent[position] // parts).reshape((-1,) + (1,) * (len(extent) - position - 1))

    level = one(*split[0])
    for cut in split[1:]:
        level = level * one(*cut)
    return level


def centred(own_key, extent, deviation, most, split=(), kind=jnp.bfloat16):
    loudness = block_scale(own_key, extent, split, -0.22, 0.18) if split else 1.0
    drawn = jax.random.normal(own_key, extent, jnp.float32) * deviation * loudness
    return jnp.minimum(jnp.maximum(drawn, -most), most).astype(kind)


def setup_inputs(seed: int = 0) -> dict:
    key_list = jax.random.split(jax.random.key(seed), 6)
    return {
        "table": draw_table(jax.random.fold_in(key_list[5], 71), 0),
        "hidden": draw_hidden(jax.random.fold_in(key_list[5], 71), 0),
        "neg_ids": place_ends(jax.random.randint(key_list[2], (N_DP, N_TABLE, N_DP, NEG_PEER), 0, ROWS_DEV), jax.random.fold_in(key_list[2], 1), 0, ROWS_DEV - 1).astype(jnp.int32),
        "pos_ids": place_ends(jax.random.randint(key_list[3], (ROWS,), 0, POOL), jax.random.fold_in(key_list[3], 1), 0, POOL - 1).astype(jnp.int32),
        "dloss": centred(key_list[4], (ROWS,), 1.0, 4.0, ((0, 32),), jnp.float32),
    }


def reference(table, hidden, neg_ids, pos_ids, dloss):
    logit_scale = 3.0 / math.sqrt(D)
    owners = (jnp.arange(N_DP, dtype=jnp.int32)[:, None] * N_TABLE + jnp.arange(N_TABLE, dtype=jnp.int32)[None, :]).astype(jnp.int32)
    grad_table = jnp.zeros(table.shape, jnp.float32)
    loss_list = []
    grad_list = []
    for group_index in range(N_DP):
        local_ids = neg_ids[:, :, group_index, :]
        global_rows = owners[:, :, None] * ROWS_DEV + local_ids
        global_rows = jnp.transpose(global_rows, (1, 0, 2)).reshape(-1).astype(jnp.int32)
        candidates = table[global_rows]
        group_hidden = hidden[group_index * GROUP_ROWS:(group_index + 1) * GROUP_ROWS]
        targets = pos_ids[group_index * GROUP_ROWS:(group_index + 1) * GROUP_ROWS]
        weights = dloss[group_index * GROUP_ROWS:(group_index + 1) * GROUP_ROWS]
        logits = logit_scale * lax.dot_general(group_hidden, candidates, (((1,), (1,)), ((), ())), precision=lax.Precision.HIGHEST, preferred_element_type=jnp.float32)
        row_max = lax.optimization_barrier(jnp.max(logits, axis=1))
        exponent = jnp.exp(logits - row_max[:, None])
        row_total = lax.optimization_barrier(jnp.sum(exponent, axis=1))
        onehot = (jnp.arange(POOL, dtype=jnp.int32)[None, :] == targets[:, None]).astype(jnp.float32)
        target_logit = lax.optimization_barrier(jnp.sum(logits * onehot, axis=1))
        loss_list.append(row_max + jnp.log(row_total) - target_logit)
        coefficient = logit_scale * weights[:, None] * (exponent / row_total[:, None] - onehot)
        grad_list.append(jnp.dot(coefficient, candidates, precision=lax.Precision.HIGHEST, preferred_element_type=jnp.float32))
        cand_grad = lax.dot_general(coefficient, group_hidden, (((0,), (0,)), ((), ())), precision=lax.Precision.HIGHEST, preferred_element_type=jnp.float32)
        grad_table = grad_table.at[global_rows].add(cand_grad)
    return (jnp.concatenate(loss_list), jnp.concatenate(grad_list, axis=0), grad_table)
```

```python
import math

import jax
import jax.numpy as jnp
from jax import lax
from jax.sharding import PartitionSpec as P


def local(table, hidden, neg_ids, pos_ids, dloss):
    feat_width = hidden.shape[1]
    logit_scale = 3.0 / math.sqrt(feat_width)
    dp_peers = lax.axis_size("dp")
    local_ids = neg_ids[0, 0]
    per_peer = local_ids.shape[1]
    local_count = dp_peers * per_peer
    outgoing = table[local_ids.reshape(-1)].reshape(dp_peers, per_peer, feat_width)
    own = lax.all_to_all(outgoing, "dp", split_axis=0, concat_axis=0, tiled=True).reshape(
        local_count, feat_width
    )
    candidates = lax.all_gather(own, "table", axis=0, tiled=True)
    pool = candidates.shape[0]
    high = dict(precision=lax.Precision.HIGH, preferred_element_type=jnp.float32)
    logits = logit_scale * lax.dot_general(hidden, candidates, (((1,), (1,)), ((), ())), **high)
    hits = lax.iota(jnp.int32, pool)[None, :] == pos_ids[:, None]
    target_logit = jnp.sum(jnp.where(hits, logits, 0.0), axis=1)
    row_max = jnp.max(logits, axis=1)
    exponent = jnp.exp(logits - row_max[:, None])
    row_total = jnp.sum(exponent, axis=1)
    row_loss = row_max + jnp.log(row_total) - target_logit
    coefficient = (
        logit_scale * dloss[:, None] * (exponent / row_total[:, None] - hits.astype(jnp.float32))
    )
    cand_grad = lax.dot_general(coefficient, hidden, (((0,), (0,)), ((), ())), **high)
    reduced = lax.psum_scatter(cand_grad, "table", scatter_dimension=0, tiled=True)
    grad_hidden = jnp.dot(coefficient, candidates, **high)
    returned = lax.all_to_all(
        reduced.reshape(dp_peers, per_peer, feat_width),
        "dp",
        split_axis=0,
        concat_axis=0,
        tiled=True,
    )
    grad_table = (
        jnp.zeros(table.shape, jnp.float32)
        .at[local_ids.reshape(-1)]
        .add(returned.reshape(local_count, feat_width))
    )
    return (row_loss, grad_hidden, grad_table)


def solution(mesh):
    in_specs = (
        P(("dp", "table"), None),
        P(("dp", "table"), None),
        P("dp", "table", None, None),
        P(("dp", "table")),
        P(("dp", "table")),
    )
    out_specs = (P(("dp", "table")), P(("dp", "table"), None), P(("dp", "table"), None))
    return jax.shard_map(local, mesh=mesh, in_specs=in_specs, out_specs=out_specs, check_vma=False)
```

```python
import functools
import math

import jax
import jax.numpy as jnp
from jax import lax
from jax.experimental import pallas as pl
from jax.experimental.pallas import tpu as pltpu
from jax.sharding import PartitionSpec as P

MESH = pl.DeviceIdType.MESH


def split(x):
    high = x.astype(jnp.bfloat16)
    return high, (x - high.astype(jnp.float32)).astype(jnp.bfloat16)


def kernel(
    peers, near, scale, piece,
    out_ref, hid_ref, side_ref,
    loss_ref, gh_ref, back_ref,
    cand, ct_hi, ct_lo, hid, h_hi, h_lo, side, expo, bstat, stat, cg, xrecv, ret, ght, ghrecv,
    local_sem, c_send, c_recv, r_send, r_recv, h_send, h_recv, d_send, d_recv,
    t_send, t_recv, x_send, x_recv, z_send, z_recv, g_send, g_recv,
):
    me = lax.axis_index("dp")
    t = lax.axis_index("table")
    hi, lo, s = t // (near * 2), lax.rem(t // 2, near), lax.rem(t, 2)
    rows, width = hid_ref.shape
    per = out_ref.shape[1]
    count = peers * per
    group = piece // per
    subs = peers // group

    def place(far, mid, last):
        return far * (near * 2) + mid * 2 + last

    def owner(dh, dg):
        return (lax.rem(me + dg, peers), place(lax.rem(hi + dh, 2), lo, s))

    def across(da):
        return (me, place(hi, lax.rem(lo + da, near), s))

    beside = (me, place(hi, lo, 1 - s))
    reach = [(dh, dg) for dh in (1, 0) for dg in range(peers) if (dh, dg) != (0, 0)]

    barrier = pltpu.get_barrier_semaphore()
    others = [owner(*r) for r in reach] + [across(da) for da in range(1, near)] + [beside]
    for other in others:
        pl.semaphore_signal(barrier, inc=1, device_id=other, device_id_type=MESH)
    pl.semaphore_wait(barrier, len(others))

    started = []

    def send(src, dst, ssem, rsem, dev):
        copy = pltpu.make_async_remote_copy(
            src_ref=src, dst_ref=dst, send_sem=ssem, recv_sem=rsem, device_id=dev, device_id_type=MESH
        )
        copy.start()
        started.append(copy)
        return copy

    own_copy = pltpu.make_async_copy(out_ref.at[me], cand.at[0, 0, me], local_sem)
    own_copy.start()
    first = {}
    for dh, dg in reach:
        first[dh, dg] = send(
            out_ref.at[lax.rem(me + dg, peers)], cand.at[dh, 0, me],
            c_send.at[dh, dg], c_recv.at[dh, dg], owner(dh, dg),
        )
    hids = []
    for da in range(1, near):
        hids.append(send(side_ref, side.at[lo], d_send.at[da], d_recv.at[da], across(da)))
        hids.append(send(hid_ref, hid.at[da - 1], h_send.at[da], h_recv.at[da], across(da)))

    side[lo] = side_ref[...]
    top, low = split(hid_ref[...])
    h_hi[lo] = top
    h_lo[lo] = low
    ght[...] = jnp.zeros_like(ght)

    relays = {}

    def relay(dh):
        for dg in range(peers):
            source = lax.rem(me + peers - dg, peers)
            if (dh, dg) == (0, 0):
                own_copy.wait()
            else:
                first[dh, dg].wait_recv()
            relays[dh, dg] = send(
                cand.at[dh, 0, source], cand.at[dh, 1, source],
                r_send.at[dh, dg], r_recv.at[dh, dg], beside,
            )

    def hits(dh, ds, j, mid):
        base = place(lax.rem(hi + dh, 2), lo, lax.rem(s + ds, 2)) * count + j * piece
        index = lax.broadcasted_iota(jnp.int32, (piece, rows), 0) + base
        return index == side[mid, 0:1, :].astype(jnp.int32)

    def forward(dh, ds):
        for j in range(subs):
            block = cand[dh, ds, j * group : (j + 1) * group].reshape(piece, width)
            b_hi, b_lo = split(block)
            turned = split(block.T)
            ct_hi[dh, ds, j] = turned[0]
            ct_lo[dh, ds, j] = turned[1]
            left = jnp.concatenate([b_hi, b_lo, b_hi], axis=1)

            def step(mid, carry):
                right = jnp.concatenate([h_hi[mid], h_hi[mid], h_lo[mid]], axis=1)
                logits = scale * lax.dot_general(
                    left, right, (((1,), (1,)), ((), ())), preferred_element_type=jnp.float32
                )
                peak = jnp.max(logits, axis=0, keepdims=True)
                power = jnp.exp(logits - peak)
                expo[dh, ds, j, mid] = power
                bstat[dh, ds, j, mid, 0:1, :] = peak
                bstat[dh, ds, j, mid, 1:2, :] = jnp.sum(power, axis=0, keepdims=True)
                bstat[dh, ds, j, mid, 2:3, :] = jnp.sum(
                    jnp.where(hits(dh, ds, j, mid), logits, 0.0), axis=0, keepdims=True
                )
                return carry

            lax.fori_loop(0, near, step, 0)

    def wait_relays(dh):
        for dg in range(peers):
            relays[dh, dg].wait_recv()

    relay(0)
    for copy in hids:
        copy.wait_recv()
    for da in range(1, near):
        mid = lax.rem(lo + near - da, near)
        top, low = split(hid[da - 1])
        h_hi[mid] = top
        h_lo[mid] = low
    forward(0, 0)
    wait_relays(0)
    relay(1)
    forward(0, 1)
    forward(1, 0)
    wait_relays(1)
    forward(1, 1)

    parts = [(dh, ds, j) for dh in (0, 1) for ds in (0, 1) for j in range(subs)]

    def gather_stats(mid, carry):
        peak = bstat[0, 0, 0, mid, 0:1, :]
        for p in parts[1:]:
            peak = jnp.maximum(peak, bstat[p[0], p[1], p[2], mid, 0:1, :])
        total = jnp.zeros_like(peak)
        target = jnp.zeros_like(peak)
        for p in parts:
            total += bstat[p[0], p[1], p[2], mid, 1:2, :] * jnp.exp(
                bstat[p[0], p[1], p[2], mid, 0:1, :] - peak
            )
            target += bstat[p[0], p[1], p[2], mid, 2:3, :]
        stat[lo, mid] = jnp.concatenate([peak, total, target] + [target] * 5, axis=0)
        return carry

    lax.fori_loop(0, near, gather_stats, 0)
    talks = [
        send(stat.at[lo], stat.at[lo], t_send.at[da], t_recv.at[da], across(da))
        for da in range(1, near)
    ]
    for copy in talks:
        copy.wait_recv()

    def merged(mid):
        peak = stat[0, mid, 0:1, :]
        for a in range(1, near):
            peak = jnp.maximum(peak, stat[a, mid, 0:1, :])
        total = jnp.zeros_like(peak)
        target = jnp.zeros_like(peak)
        for a in range(near):
            total += stat[a, mid, 1:2, :] * jnp.exp(stat[a, mid, 0:1, :] - peak)
            target += stat[a, mid, 2:3, :]
        return peak, total, target

    peak, total, target = merged(lo)
    loss_ref[...] = peak + jnp.log(total) - target

    def backward(dh, ds):
        for j in range(subs):
            flip = jnp.concatenate([ct_hi[dh, ds, j], ct_hi[dh, ds, j], ct_lo[dh, ds, j]], axis=1)

            def step(mid, acc):
                peak, total, _ = merged(mid)
                weight = scale * side[mid, 1:2, :]
                factor = weight * jnp.exp(bstat[dh, ds, j, mid, 0:1, :] - peak) / total
                power = expo[dh, ds, j, mid] * factor
                c_hi, c_lo = split(jnp.where(hits(dh, ds, j, mid), power - weight, power))
                ght[mid] += jnp.dot(
                    flip, jnp.concatenate([c_hi, c_lo, c_hi], axis=0),
                    preferred_element_type=jnp.float32,
                )
                return acc + jnp.dot(
                    jnp.concatenate([c_hi, c_lo, c_hi], axis=1),
                    jnp.concatenate([h_hi[mid], h_hi[mid], h_lo[mid]], axis=0),
                    preferred_element_type=jnp.float32,
                )

            acc = lax.fori_loop(0, near, step, jnp.zeros((piece, width), jnp.float32))
            cg[dh, ds, j * group : (j + 1) * group] = acc.reshape(group, per, width)

    sides = {}

    def send_side(dh):
        for dg in range(peers):
            source = lax.rem(me + dg, peers)
            sides[dh, dg] = send(
                cg.at[dh, 1, source], xrecv.at[dh, source],
                x_send.at[dh, dg], x_recv.at[dh, dg], beside,
            )

    finals = []

    def finish(dh, first_dg, last_dg):
        for dg in range(first_dg, last_dg):
            source = lax.rem(me + dg, peers)
            sides[dh, dg].wait_recv()
            value = cg[dh, 0, source] + xrecv[dh, source]
            if (dh, dg) == (0, 0):
                ret[0, me] = value
            else:
                cg[dh, 0, source] = value
                finals.append(
                    send(
                        cg.at[dh, 0, source], ret.at[dh, me],
                        z_send.at[dh, dg], z_recv.at[dh, dg], owner(dh, dg),
                    )
                )

    backward(1, 1)
    send_side(1)
    backward(1, 0)
    backward(0, 1)
    send_side(0)
    finish(1, 0, peers // 2)
    backward(0, 0)
    grads = [
        send(ght.at[lax.rem(lo + da, near)], ghrecv.at[da - 1], g_send.at[da], g_recv.at[da], across(da))
        for da in range(1, near)
    ]
    finish(1, peers // 2, peers)
    finish(0, 0, peers)
    for copy in grads:
        copy.wait_recv()
    whole = ght[lo]
    for da in range(1, near):
        whole += ghrecv[da - 1]
    gh_ref[...] = whole.T
    for copy in finals:
        copy.wait_recv()
    back_ref[...] = ret[0] + ret[1]
    for copy in started:
        copy.wait_send()


def local(table, hidden, neg_ids, pos_ids, dloss):
    rows, width = hidden.shape
    scale = 3.0 / math.sqrt(width)
    peers = lax.axis_size("dp")
    near = lax.axis_size("table") // 4
    flat_ids = neg_ids[0, 0].reshape(-1)
    per = neg_ids.shape[3]
    count = peers * per
    piece = math.gcd(512, count)
    subs = count // piece
    outgoing = table.at[flat_ids].get(mode="promise_in_bounds").reshape(peers, per, width)
    side = jnp.stack([pos_ids.astype(jnp.float32), dloss] + [dloss] * 6, axis=0)
    f32, bf16 = jnp.float32, jnp.bfloat16
    pairs = pltpu.SemaphoreType.DMA((2, peers))
    nears = pltpu.SemaphoreType.DMA((near,))
    vmem = pl.BlockSpec(memory_space=pltpu.VMEM)
    flops = 18 * 4 * count * near * rows * width
    loss, grad_hidden, returned = pl.pallas_call(
        functools.partial(kernel, peers, near, scale, piece),
        out_shape=(
            jax.ShapeDtypeStruct((1, rows), f32),
            jax.ShapeDtypeStruct((rows, width), f32),
            jax.ShapeDtypeStruct((peers, per, width), f32),
        ),
        in_specs=[vmem] * 3,
        out_specs=(vmem,) * 3,
        scratch_shapes=[
            pltpu.VMEM((2, 2, peers, per, width), f32),
            pltpu.VMEM((2, 2, subs, width, piece), bf16),
            pltpu.VMEM((2, 2, subs, width, piece), bf16),
            pltpu.VMEM((max(near - 1, 1), rows, width), f32),
            pltpu.VMEM((near, rows, width), bf16),
            pltpu.VMEM((near, rows, width), bf16),
            pltpu.VMEM((near, 8, rows), f32),
            pltpu.VMEM((2, 2, subs, near, piece, rows), f32),
            pltpu.VMEM((2, 2, subs, near, 8, rows), f32),
            pltpu.VMEM((near, near, 8, rows), f32),
            pltpu.VMEM((2, 2, peers, per, width), f32),
            pltpu.VMEM((2, peers, per, width), f32),
            pltpu.VMEM((2, peers, per, width), f32),
            pltpu.VMEM((near, width, rows), f32),
            pltpu.VMEM((max(near - 1, 1), width, rows), f32),
            pltpu.SemaphoreType.DMA,
            pairs, pairs, pairs, pairs, nears, nears, nears, nears,
            nears, nears, pairs, pairs, pairs, pairs, nears, nears,
        ],
        compiler_params=pltpu.CompilerParams(
            collective_id=0, has_side_effects=True, vmem_limit_bytes=67043328
        ),
        cost_estimate=pl.CostEstimate(flops=flops, bytes_accessed=4 * count * width, transcendentals=0),
    )(outgoing, hidden, side)
    grad_table = (
        jnp.zeros(table.shape, f32)
        .at[flat_ids]
        .add(returned.reshape(count, width), mode="promise_in_bounds")
    )
    return (loss.reshape(rows), grad_hidden, grad_table)


def solution(mesh):
    in_specs = (
        P(("dp", "table"), None),
        P(("dp", "table"), None),
        P("dp", "table", None, None),
        P(("dp", "table")),
        P(("dp", "table")),
    )
    out_specs = (P(("dp", "table")), P(("dp", "table"), None), P(("dp", "table"), None))
    return jax.shard_map(local, mesh=mesh, in_specs=in_specs, out_specs=out_specs, check_vma=False)
```

```python
import functools
import math

import jax
import jax.numpy as jnp
from jax import lax
from jax.experimental import pallas as pl
from jax.experimental.pallas import tpu as pltpu
from jax.sharding import PartitionSpec as P

MESH = pl.DeviceIdType.MESH


def split(x):
    high = x.astype(jnp.bfloat16)
    return high, (x - high.astype(jnp.float32)).astype(jnp.bfloat16)


def kernel(
    peers, near, scale, piece,
    out_ref, hid_ref, side_ref,
    loss_ref, gh_ref, back_ref,
    cand, ct_hi, ct_lo, hid, h_hi, h_lo, side, expo, bstat, stat, cg, xrecv, ret, ght, ghrecv,
    local_sem, c_send, c_recv, r_send, r_recv, h_send, h_recv, d_send, d_recv,
    t_send, t_recv, x_send, x_recv, z_send, z_recv, g_send, g_recv,
):
    me = lax.axis_index("dp")
    t = lax.axis_index("table")
    hi, lo, s = t // (near * 2), lax.rem(t // 2, near), lax.rem(t, 2)
    rows, width = hid_ref.shape
    per = out_ref.shape[1]
    count = peers * per
    group = piece // per
    subs = peers // group

    def place(far, mid, last):
        return far * (near * 2) + mid * 2 + last

    def owner(dh, dg):
        return (lax.rem(me + dg, peers), place(lax.rem(hi + dh, 2), lo, s))

    def across(da):
        return (me, place(hi, lax.rem(lo + da, near), s))

    beside = (me, place(hi, lo, 1 - s))
    reach = [(dh, dg) for dh in (0, 1) for dg in range(peers) if (dh, dg) != (0, 0)]

    barrier = pltpu.get_barrier_semaphore()
    others = [owner(*r) for r in reach] + [across(da) for da in range(1, near)] + [beside]
    for other in others:
        pl.semaphore_signal(barrier, inc=1, device_id=other, device_id_type=MESH)
    pl.semaphore_wait(barrier, len(others))

    started = []

    def send(src, dst, ssem, rsem, dev):
        copy = pltpu.make_async_remote_copy(
            src_ref=src, dst_ref=dst, send_sem=ssem, recv_sem=rsem, device_id=dev, device_id_type=MESH
        )
        copy.start()
        started.append(copy)
        return copy

    own_copy = pltpu.make_async_copy(out_ref.at[me], cand.at[0, 0, me], local_sem)
    own_copy.start()
    first = {}
    hids = []

    def push(far):
        for dh, dg in reach:
            if dh == far:
                first[dh, dg] = send(
                    out_ref.at[lax.rem(me + dg, peers)], cand.at[dh, 0, me],
                    c_send.at[dh, dg], c_recv.at[dh, dg], owner(dh, dg),
                )

    push(0)
    for da in range(1, near):
        hids.append(send(side_ref, side.at[lo], d_send.at[da], d_recv.at[da], across(da)))
        hids.append(send(hid_ref, hid.at[da - 1], h_send.at[da], h_recv.at[da], across(da)))
    push(1)

    side[lo] = side_ref[...]
    top, low = split(hid_ref[...])
    h_hi[lo] = top
    h_lo[lo] = low
    ght[...] = jnp.zeros_like(ght)

    relays = {}

    def relay(dh, first_dg, last_dg):
        for dg in range(first_dg, last_dg):
            source = lax.rem(me + peers - dg, peers)
            if (dh, dg) == (0, 0):
                own_copy.wait()
            else:
                first[dh, dg].wait_recv()
            relays[dh, dg] = send(
                cand.at[dh, 0, source], cand.at[dh, 1, source],
                r_send.at[dh, dg], r_recv.at[dh, dg], beside,
            )

    def hits(dh, ds, j, mid):
        base = place(lax.rem(hi + dh, 2), lo, lax.rem(s + ds, 2)) * count + j * piece
        index = lax.broadcasted_iota(jnp.int32, (piece, rows), 0) + base
        return index == side[mid, 0:1, :].astype(jnp.int32)

    def forward(dh, ds):
        for j in range(subs):
            block = cand[dh, ds, j * group : (j + 1) * group].reshape(piece, width)
            b_hi, b_lo = split(block)
            turned = split(block.T)
            ct_hi[dh, ds, j] = turned[0]
            ct_lo[dh, ds, j] = turned[1]
            left = jnp.concatenate([b_hi, b_lo, b_hi], axis=1)

            def step(mid, carry):
                right = jnp.concatenate([h_hi[mid], h_hi[mid], h_lo[mid]], axis=1)
                logits = scale * lax.dot_general(
                    left, right, (((1,), (1,)), ((), ())), preferred_element_type=jnp.float32
                )
                peak = jnp.max(logits, axis=0, keepdims=True)
                power = jnp.exp(logits - peak)
                expo[dh, ds, j, mid] = power
                bstat[dh, ds, j, mid, 0:1, :] = peak
                bstat[dh, ds, j, mid, 1:2, :] = jnp.sum(power, axis=0, keepdims=True)
                bstat[dh, ds, j, mid, 2:3, :] = jnp.sum(
                    jnp.where(hits(dh, ds, j, mid), logits, 0.0), axis=0, keepdims=True
                )
                return carry

            lax.fori_loop(0, near, step, 0)

    def wait_relays(dh):
        for dg in range(peers):
            relays[dh, dg].wait_recv()

    relay(0, 0, peers)
    for copy in hids:
        copy.wait_recv()
    for da in range(1, near):
        mid = lax.rem(lo + near - da, near)
        top, low = split(hid[da - 1])
        h_hi[mid] = top
        h_lo[mid] = low
    forward(0, 0)
    relay(1, 0, peers // 2)
    wait_relays(0)
    forward(0, 1)
    relay(1, peers // 2, peers)
    forward(1, 0)
    wait_relays(1)
    forward(1, 1)

    parts = [(dh, ds, j) for dh in (0, 1) for ds in (0, 1) for j in range(subs)]

    def gather_stats(mid, carry):
        peak = bstat[0, 0, 0, mid, 0:1, :]
        for p in parts[1:]:
            peak = jnp.maximum(peak, bstat[p[0], p[1], p[2], mid, 0:1, :])
        total = jnp.zeros_like(peak)
        target = jnp.zeros_like(peak)
        for p in parts:
            total += bstat[p[0], p[1], p[2], mid, 1:2, :] * jnp.exp(
                bstat[p[0], p[1], p[2], mid, 0:1, :] - peak
            )
            target += bstat[p[0], p[1], p[2], mid, 2:3, :]
        stat[lo, mid] = jnp.concatenate([peak, total, target] + [target] * 5, axis=0)
        return carry

    lax.fori_loop(0, near, gather_stats, 0)
    talks = [
        send(stat.at[lo], stat.at[lo], t_send.at[da], t_recv.at[da], across(da))
        for da in range(1, near)
    ]
    for copy in talks:
        copy.wait_recv()

    def merged(mid):
        peak = stat[0, mid, 0:1, :]
        for a in range(1, near):
            peak = jnp.maximum(peak, stat[a, mid, 0:1, :])
        total = jnp.zeros_like(peak)
        target = jnp.zeros_like(peak)
        for a in range(near):
            total += stat[a, mid, 1:2, :] * jnp.exp(stat[a, mid, 0:1, :] - peak)
            target += stat[a, mid, 2:3, :]
        return peak, total, target

    peak, total, target = merged(lo)
    loss_ref[...] = peak + jnp.log(total) - target

    def backward(dh, ds):
        for j in range(subs):
            flip = jnp.concatenate([ct_hi[dh, ds, j], ct_hi[dh, ds, j], ct_lo[dh, ds, j]], axis=1)

            def step(mid, acc):
                peak, total, _ = merged(mid)
                weight = scale * side[mid, 1:2, :]
                factor = weight * jnp.exp(bstat[dh, ds, j, mid, 0:1, :] - peak) / total
                power = expo[dh, ds, j, mid] * factor
                c_hi, c_lo = split(jnp.where(hits(dh, ds, j, mid), power - weight, power))
                ght[mid] += jnp.dot(
                    flip, jnp.concatenate([c_hi, c_lo, c_hi], axis=0),
                    preferred_element_type=jnp.float32,
                )
                return acc + jnp.dot(
                    jnp.concatenate([c_hi, c_lo, c_hi], axis=1),
                    jnp.concatenate([h_hi[mid], h_hi[mid], h_lo[mid]], axis=0),
                    preferred_element_type=jnp.float32,
                )

            acc = lax.fori_loop(0, near, step, jnp.zeros((piece, width), jnp.float32))
            cg[dh, ds, j * group : (j + 1) * group] = acc.reshape(group, per, width)

    sides = {}

    def send_side(dh):
        for dg in range(peers):
            source = lax.rem(me + dg, peers)
            sides[dh, dg] = send(
                cg.at[dh, 1, source], xrecv.at[dh, source],
                x_send.at[dh, dg], x_recv.at[dh, dg], beside,
            )

    finals = []

    def finish(dh, first_dg, last_dg):
        for dg in range(first_dg, last_dg):
            source = lax.rem(me + dg, peers)
            sides[dh, dg].wait_recv()
            value = cg[dh, 0, source] + xrecv[dh, source]
            if (dh, dg) == (0, 0):
                ret[0, me] = value
            else:
                cg[dh, 0, source] = value
                finals.append(
                    send(
                        cg.at[dh, 0, source], ret.at[dh, me],
                        z_send.at[dh, dg], z_recv.at[dh, dg], owner(dh, dg),
                    )
                )

    backward(1, 1)
    send_side(1)
    backward(1, 0)
    backward(0, 1)
    send_side(0)
    finish(1, 0, peers // 2)
    backward(0, 0)
    grads = [
        send(ght.at[lax.rem(lo + da, near)], ghrecv.at[da - 1], g_send.at[da], g_recv.at[da], across(da))
        for da in range(1, near)
    ]
    finish(1, peers // 2, peers)
    finish(0, 0, peers)
    for copy in grads:
        copy.wait_recv()
    whole = ght[lo]
    for da in range(1, near):
        whole += ghrecv[da - 1]
    gh_ref[...] = whole.T
    for copy in finals:
        copy.wait_recv()
    back_ref[...] = ret[0] + ret[1]
    for copy in started:
        copy.wait_send()


def local(table, hidden, neg_ids, pos_ids, dloss):
    rows, width = hidden.shape
    scale = 3.0 / math.sqrt(width)
    peers = lax.axis_size("dp")
    near = lax.axis_size("table") // 4
    flat_ids = neg_ids[0, 0].reshape(-1)
    per = neg_ids.shape[3]
    count = peers * per
    piece = math.gcd(512, count)
    subs = count // piece
    outgoing = table.at[flat_ids].get(mode="promise_in_bounds").reshape(peers, per, width)
    side = jnp.stack([pos_ids.astype(jnp.float32), dloss] + [dloss] * 6, axis=0)
    f32, bf16 = jnp.float32, jnp.bfloat16
    pairs = pltpu.SemaphoreType.DMA((2, peers))
    nears = pltpu.SemaphoreType.DMA((near,))
    vmem = pl.BlockSpec(memory_space=pltpu.VMEM)
    flops = 18 * 4 * count * near * rows * width
    loss, grad_hidden, returned = pl.pallas_call(
        functools.partial(kernel, peers, near, scale, piece),
        out_shape=(
            jax.ShapeDtypeStruct((1, rows), f32),
            jax.ShapeDtypeStruct((rows, width), f32),
            jax.ShapeDtypeStruct((peers, per, width), f32),
        ),
        in_specs=[vmem] * 3,
        out_specs=(vmem,) * 3,
        scratch_shapes=[
            pltpu.VMEM((2, 2, peers, per, width), f32),
            pltpu.VMEM((2, 2, subs, width, piece), bf16),
            pltpu.VMEM((2, 2, subs, width, piece), bf16),
            pltpu.VMEM((max(near - 1, 1), rows, width), f32),
            pltpu.VMEM((near, rows, width), bf16),
            pltpu.VMEM((near, rows, width), bf16),
            pltpu.VMEM((near, 8, rows), f32),
            pltpu.VMEM((2, 2, subs, near, piece, rows), f32),
            pltpu.VMEM((2, 2, subs, near, 8, rows), f32),
            pltpu.VMEM((near, near, 8, rows), f32),
            pltpu.VMEM((2, 2, peers, per, width), f32),
            pltpu.VMEM((2, peers, per, width), f32),
            pltpu.VMEM((2, peers, per, width), f32),
            pltpu.VMEM((near, width, rows), f32),
            pltpu.VMEM((max(near - 1, 1), width, rows), f32),
            pltpu.SemaphoreType.DMA,
            pairs, pairs, pairs, pairs, nears, nears, nears, nears,
            nears, nears, pairs, pairs, pairs, pairs, nears, nears,
        ],
        compiler_params=pltpu.CompilerParams(
            collective_id=0, has_side_effects=True, vmem_limit_bytes=67043328
        ),
        cost_estimate=pl.CostEstimate(flops=flops, bytes_accessed=4 * count * width, transcendentals=0),
    )(outgoing, hidden, side)
    grad_table = (
        jnp.zeros(table.shape, f32)
        .at[flat_ids]
        .add(returned.reshape(count, width), mode="promise_in_bounds")
    )
    return (loss.reshape(rows), grad_hidden, grad_table)


def solution(mesh):
    in_specs = (
        P(("dp", "table"), None),
        P(("dp", "table"), None),
        P("dp", "table", None, None),
        P(("dp", "table")),
        P(("dp", "table")),
    )
    out_specs = (P(("dp", "table")), P(("dp", "table"), None), P(("dp", "table"), None))
    return jax.shard_map(local, mesh=mesh, in_specs=in_specs, out_specs=out_specs, check_vma=False)
```
